768 devices in a mesh: dp: 24 (over x_hi, z), fsdp: 16 (over y, core), query: 2 (over x_lo).
Axes of the slice: x: 4 (x_hi: 2, x_lo: 2; x = x_hi * 2 + x_lo), y: 8, z: 12, core: 2. Of those that a mesh axis runs over, the one named last changes fastest.
Arguments:
- queries: bfloat16 [16, 6144, 1024], P('fsdp', ('dp', 'query')), may hold values from -40 to 40
- passages: bfloat16 [16, 12288, 1024], P('fsdp', ('dp', 'query')), may hold values from -6 to 6
- head_weight: bfloat16 [1024, 1024], P('fsdp'), may hold values from -0.1875 to 0.1875
- positives: int32 [16, 6144], P('fsdp', ('dp', 'query')), may hold values from 0 to 12287
- negative_ids: int32 [16, 48, 12], P('fsdp', ('dp', 'query')), may hold values from 0 to 95, as said below
- negative_count: int32 [16, 48], P('fsdp', ('dp', 'query')), may hold values from 4 to 12, as said below
Outputs:
- query_loss: float32 [16, 6144], P('fsdp', ('dp', 'query'))
The draws below stay inside these ranges and needn't reach their ends.
Inputs may be any that keep to these rules, and one draw needn't show every extreme that they name: `negative_ids`: the 12 entries of a query block are distinct passage blocks of its index shard; only the first negative_count of them are live. `negative_count`: in every aligned run of 8 query blocks one has exactly 12 live entries.
All inputs are finite; a program needn't handle non-finite values.
Results may differ from the reference program's by a relative error of at most 0.0048.
Values may be sent and summed in bfloat16 or wider, within the bound.
No kernel may reach another device: no remote copies, remote signals or barrier semaphores. Data moves between devices by JAX's collectives and lax.ppermute only.
A program may use at most 64 MiB of HBM per device.

```python
import jax
import jax.numpy as jnp
from jax import lax

E = 1024
BLOCK = 128
COLUMNS = 16
QCOL = 6144
CROWS = 12288
NQB = 48
NBC = 96
MAXL = 12


def list_draw(key):
    key_order, key_count, key_full, key_pos = jax.random.split(jax.random.fold_in(key, 101), 4)
    raw_scores = jax.random.randint(key_order, (COLUMNS, NQB, NBC), 0, 1 << 20)
    distinct = raw_scores * NBC + lax.broadcasted_iota(jnp.int32, (COLUMNS, NQB, NBC), 2)
    ordering = jnp.argsort(distinct, axis=2, stable=True).astype(jnp.int32)
    list_ids = ordering[:, :, :MAXL]
    least = (MAXL + 2) // 3
    counts = jax.random.randint(key_count, (COLUMNS, NQB), least, MAXL + 1)
    group_len = 8
    picked = jax.random.randint(key_full, (COLUMNS, NQB // group_len), 0, group_len)
    position = lax.broadcasted_iota(jnp.int32, (COLUMNS, NQB), 1) % group_len
    counts = jnp.where(position == jnp.repeat(picked, group_len, axis=1), MAXL, counts)
    targets = jax.random.randint(key_pos, (COLUMNS, QCOL), 0, CROWS)
    return (list_ids, counts.astype(jnp.int32), targets.astype(jnp.int32))


def float_draw(key):
    list_ids, counts, targets = list_draw(key)
    key_pas = jax.random.fold_in(jax.random.fold_in(key, 202), 0)
    key_que = jax.random.fold_in(jax.random.fold_in(key, 202), 1)
    key_pick = jax.random.fold_in(jax.random.fold_in(key, 202), 3)
    key_sign = jax.random.fold_in(jax.random.fold_in(key, 202), 4)
    key_dir = jax.random.fold_in(jax.random.fold_in(key, 202), 5)
    key_lift = jax.random.fold_in(jax.random.fold_in(key, 202), 6)
    passage_vals = jax.random.truncated_normal(key_pas, -4.0, 4.0, (COLUMNS, CROWS, E), jnp.float32)
    noise_vals = jax.random.truncated_normal(key_que, -6.0, 6.0, (COLUMNS, QCOL, E), jnp.float32)
    shared_dir = (jax.random.randint(key_dir, (COLUMNS, E), 0, 2) * 2 - 1).astype(jnp.float32)
    passage_vals = passage_vals + 2.0 * shared_dir[:, None, :]
    lift = jax.random.uniform(key_lift, (COLUMNS, QCOL, 1), jnp.float32, 0.0, 3.0)
    matched = jax.vmap(lambda table, index: table[index])(passage_vals, targets)
    query_vals = 0.3 * matched + noise_vals + lift * shared_dir[:, None, :]
    column_ids = jnp.arange(COLUMNS, dtype=jnp.int32)
    level = jnp.array([120.0, 180.0, 240.0], jnp.float32)[column_ids % 3]
    chosen_block = jax.random.randint(key_pick, (COLUMNS,), 0, NQB)
    query_row = chosen_block * BLOCK
    source_row = targets[column_ids, query_row]
    target_row = list_ids[column_ids, chosen_block, 0] * BLOCK + 1
    signs = (jax.random.randint(key_sign, (COLUMNS, E), 0, 2) * 2 - 1).astype(jnp.float32)
    source_vals = 3.0 * signs
    strength = level / (9.0 * E ** 0.5)
    passage_vals = passage_vals.at[column_ids, source_row].set(source_vals)
    query_vals = query_vals.at[column_ids, query_row].set(strength[:, None] * source_vals)
    shrink = 1.0 - 2.0 / level
    passage_vals = passage_vals.at[column_ids, target_row].set(shrink[:, None] * source_vals)
    return (query_vals, passage_vals)


def draw_queries(key, part):
    return float_draw(key)[0].astype(jnp.bfloat16)


def draw_passages(key, part):
    return float_draw(key)[1].astype(jnp.bfloat16)


def draw_positives(key, part):
    return list_draw(key)[2]


def draw_negative_ids(key, part):
    return list_draw(key)[0]


def draw_negative_count(key, part):
    return list_draw(key)[1]


def steps_of(rng, extent, cuts, low, top_value):
    loudness, own = 1.0, jax.random.fold_in(rng, 6)
    for axis_at, shards_of in cuts:
        draws = jnp.exp(jax.random.uniform(jax.random.fold_in(own, axis_at), (shards_of,), jnp.float32, low / len(cuts), top_value / len(cuts)))
        loudness = loudness * jnp.repeat(draws, extent[axis_at] // shards_of).reshape([-1 if axis == axis_at else 1 for axis in range(len(extent))])
    return loudness


def centred(rng, extent, width, bound, cuts=(), kind=jnp.bfloat16):
    factor_of = steps_of(rng, extent, cuts, -0.22, 0.18) if cuts else 1.0
    values = jax.random.normal(rng, extent, jnp.float32) * width * factor_of
    return jnp.minimum(jnp.maximum(values, -bound), bound).astype(kind)


def setup_inputs(seed: int = 0) -> dict:
    splits = jax.random.split(jax.random.key(seed), 7)
    return {
        "queries": draw_queries(jax.random.fold_in(splits[6], 71), 0),
        "passages": draw_passages(jax.random.fold_in(splits[6], 71), 0),
        "head_weight": centred(splits[2], (E, E), E ** -0.5, 0.1875, ((0, 16),)),
        "positives": draw_positives(jax.random.fold_in(splits[6], 71), 0),
        "negative_ids": draw_negative_ids(jax.random.fold_in(splits[6], 71), 0),
        "negative_count": draw_negative_count(jax.random.fold_in(splits[6], 71), 0),
    }


masked_floor = -1.0e30


def column_loss(queries, passages, head_weight, positives, negative_ids, negative_count):
    query_proj = jnp.dot(queries, head_weight, preferred_element_type=jnp.float32).astype(jnp.bfloat16)
    passage_proj = jnp.dot(passages, head_weight, preferred_element_type=jnp.float32).astype(jnp.bfloat16)
    scale_factor = E ** -0.5
    row_index = jnp.arange(CROWS, dtype=jnp.int32)
    live_slot = jnp.arange(MAXL, dtype=jnp.int32)[None, :] < negative_count[:, None]
    block_index = jnp.arange(NBC, dtype=jnp.int32)
    block_used = jnp.any((negative_ids[:, :, None] == block_index[None, None, :]) & live_slot[:, :, None], axis=1)

    def one_block(members):
        query_block, used_here, targets = members
        logits = jnp.dot(query_block, passage_proj.T, preferred_element_type=jnp.float32) * scale_factor
        is_target = row_index[None, :] == targets[:, None]
        chosen = jnp.repeat(used_here, BLOCK)[None, :] | is_target
        running_max = jnp.max(jnp.where(chosen, logits, masked_floor), axis=1)
        running_sum = jnp.sum(jnp.where(chosen, jnp.exp(logits - running_max[:, None]), 0.0), axis=1)
        target_logit = jnp.sum(jnp.where(is_target, logits, 0.0), axis=1)
        return running_max + jnp.log(running_sum) - target_logit

    shaped = (query_proj.reshape(NQB, BLOCK, E), block_used, positives.reshape(NQB, BLOCK))
    return lax.map(one_block, shaped).reshape(-1)


def reference(queries, passages, head_weight, positives, negative_ids, negative_count):
    def per_column(members):
        return column_loss(members[0], members[1], head_weight, members[2], members[3], members[4])

    return lax.map(per_column, (queries, passages, positives, negative_ids, negative_count))
```

```python
import functools

import jax
import jax.numpy as jnp
from jax import lax
from jax.experimental import pallas as pl
from jax.experimental.pallas import tpu as pltpu
from jax.sharding import Mesh
from jax.sharding import PartitionSpec as P

BLOCK = 128
FLOOR = -1e30
ROW = ("xh", "xl")
NT = (((1,), (1,)), ((), ()))
VMEM_BYTES = 48 * 1024 * 1024


def passage_kernel(passages, head, proj, full):
    cores, steps, depth, _ = head.shape
    for y in range(steps):
        for c in range(cores):
            full[pl.ds((y * cores + c) * depth, depth), :] = head[c, y]
    shards, rows, _ = passages.shape
    for s in range(shards):
        proj[pl.ds(s * rows, rows), :] = jnp.dot(
            passages[s], full[...], preferred_element_type=jnp.float32
        ).astype(proj.dtype)


def query_kernel(scale, used, queries, full, proj, target, out, logits):
    step = pl.program_id(0)
    query_rows = queries.shape[0]
    count = query_rows // BLOCK
    tiles = proj.shape[0] // BLOCK
    query_proj = jnp.dot(
        queries[...], full[...], preferred_element_type=jnp.float32
    ).astype(jnp.bfloat16)
    logits[...] = lax.dot_general(proj[...], query_proj, NT, preferred_element_type=jnp.float32)
    sub = lax.broadcasted_iota(jnp.int32, (BLOCK, BLOCK), 0)
    for b in range(count):
        lanes = pl.ds(b * BLOCK, BLOCK)
        wanted = target[b]
        found = jnp.zeros((BLOCK, BLOCK), jnp.float32)
        for j in range(tiles):
            tile = logits[pl.ds(j * BLOCK, BLOCK), lanes]
            found = found + jnp.where(sub == wanted - j * BLOCK, tile, 0.0)
        found = jnp.sum(found, axis=0, keepdims=True) * scale

        def peak(j, top):
            def live(top):
                tile = logits[pl.ds(pl.multiple_of(j * BLOCK, BLOCK), BLOCK), lanes]
                return jnp.maximum(top, jnp.max(tile.reshape(BLOCK // 8, 8, BLOCK), axis=0))

            return lax.cond(used[step * count + b, j] > 0, live, lambda t: t, top)

        top = lax.fori_loop(0, tiles, peak, jnp.full((8, BLOCK), FLOOR, jnp.float32))
        top = jnp.max(top, axis=0, keepdims=True)

        def total(j, acc):
            def live(acc):
                tile = logits[pl.ds(pl.multiple_of(j * BLOCK, BLOCK), BLOCK), lanes]
                part = jnp.exp((tile - top) * scale)
                return acc + jnp.sum(part.reshape(BLOCK // 8, 8, BLOCK), axis=0)

            return lax.cond(used[step * count + b, j] > 0, live, lambda t: t, acc)

        acc = lax.fori_loop(0, tiles, total, jnp.zeros((8, BLOCK), jnp.float32))
        acc = jnp.sum(acc, axis=0, keepdims=True)
        some = acc > 0.0
        lse = jnp.where(some, top * scale + jnp.log(jnp.where(some, acc, 1.0)), FLOOR)
        out[b, 0:1, :] = lse
        out[b, 1:2, :] = found


def local(queries, passages, head, positives, negative_ids, negative_count):
    queries, passages = queries[0], passages[0]
    width = queries.shape[1]
    scale = width ** (-0.5)
    deep, wide = lax.axis_size("z"), lax.axis_size(ROW)
    high = lax.axis_size("xh")
    cores, steps = lax.axis_size("core"), lax.axis_size("y")
    z = lax.axis_index("z")
    rows = passages.shape[0]

    gathered = lax.all_gather(queries, "z", axis=0, tiled=True)

    head = lax.all_to_all(jnp.broadcast_to(head, (steps,) + head.shape), "y", 0, 0)
    met = lax.all_to_all(jnp.broadcast_to(passages, (wide,) + passages.shape), ROW, 0, 0)
    head = lax.all_to_all(jnp.broadcast_to(head, (cores,) + head.shape), "core", 0, 0)

    slots = negative_ids.shape[2]
    live = lax.broadcasted_iota(jnp.int32, (1, slots), 1) < negative_count
    listed = jnp.where(live, negative_ids[0], -1)
    packed = jnp.concatenate(
        [positives, jnp.pad(listed, ((0, 0), (0, BLOCK - slots)), constant_values=-1)], axis=0
    )
    met_lists = lax.all_gather(packed, "z")
    wanted, lists = met_lists[:, 0, :], met_lists[:, 1, :slots]

    run = rows * (wide // high)
    span = run * deep
    upper = wanted // span
    inside = wanted - upper * span - z * run
    target = jnp.where((inside >= 0) & (inside < run), upper * run + inside, -1)
    tiles = rows * wide // BLOCK
    tile = lax.iota(jnp.int32, tiles)
    per_run = run // BLOCK
    tile_id = (tile // per_run) * (span // BLOCK) + z * per_run + tile % per_run
    used = jnp.any(lists[:, :, None] == tile_id[None, None, :], axis=1).astype(jnp.int32)

    vmem = pl.BlockSpec(memory_space=pltpu.VMEM)
    proj, full = pl.pallas_call(
        passage_kernel,
        out_shape=(
            jax.ShapeDtypeStruct((rows * wide, width), jnp.bfloat16),
            jax.ShapeDtypeStruct((width, width), jnp.bfloat16),
        ),
        in_specs=[vmem, vmem],
        out_specs=(vmem, vmem),
        compiler_params=pltpu.CompilerParams(vmem_limit_bytes=VMEM_BYTES),
    )(met, head)

    chunks = 3
    per = deep // chunks
    stats = pl.pallas_call(
        functools.partial(query_kernel, scale),
        out_shape=jax.ShapeDtypeStruct((deep, 2, BLOCK), jnp.float32),
        grid_spec=pltpu.PrefetchScalarGridSpec(
            num_scalar_prefetch=1,
            grid=(chunks,),
            in_specs=[
                pl.BlockSpec((per * BLOCK, width), lambda i, u: (i, 0)),
                vmem,
                vmem,
                pl.BlockSpec((per, 1, BLOCK), lambda i, u: (i, 0, 0)),
            ],
            out_specs=pl.BlockSpec((per, 2, BLOCK), lambda i, u: (i, 0, 0)),
            scratch_shapes=[pltpu.VMEM((rows * wide, per * BLOCK), jnp.float32)],
        ),
        compiler_params=pltpu.CompilerParams(vmem_limit_bytes=VMEM_BYTES),
    )(used, gathered, full, proj, target[:, None, :])

    home = lax.all_to_all(stats, "z", 0, 0)
    logit = jnp.sum(home[:, 1, :], axis=0)
    also_listed = jnp.any(listed[0][:, None] == positives // BLOCK, axis=0)
    extra = jnp.where(also_listed, FLOOR, logit)
    top = jnp.maximum(jnp.max(home[:, 0, :], axis=0), extra)
    total = jnp.sum(jnp.exp(home[:, 0, :] - top), axis=0) + jnp.exp(extra - top)
    return (top + jnp.log(total) - logit)[None, :]


def solution(mesh):
    grid = Mesh(mesh.devices.reshape(2, 12, 8, 2, 2), ("xh", "z", "y", "core", "xl"))
    shard, part = ("y", "core"), ("xh", "z", "xl")
    in_specs = (
        P(shard, part, None),
        P(shard, part, None),
        P(shard, None),
        P(shard, part),
        P(shard, part, None),
        P(shard, part),
    )
    return jax.shard_map(
        local, mesh=grid, in_specs=in_specs, out_specs=P(shard, part), check_vma=False
    )
```

```python
import functools

import jax
import jax.numpy as jnp
from jax import lax
from jax.experimental import pallas as pl
from jax.experimental.pallas import tpu as pltpu
from jax.sharding import Mesh
from jax.sharding import PartitionSpec as P

BLOCK = 128
FLOOR = -1e30
NT = (((1,), (1,)), ((), ()))
VMEM_BYTES = 24 * 1024 * 1024
PARTS = (512, 1024)


def passage_kernel(core, mine, other, *refs):
    *pieces, full, proj = refs
    steps, depth, _ = mine.shape
    here = core[0]
    for y in range(steps):
        first = pl.multiple_of((2 * y + here) * depth, depth)
        second = pl.multiple_of((2 * y + 1 - here) * depth, depth)
        full[pl.ds(first, depth), :] = mine[y]
        full[pl.ds(second, depth), :] = other[y]
    rows = pieces[0].shape[0]
    for s, piece in enumerate(pieces):
        proj[pl.ds(s * rows, rows), :] = jnp.dot(
            piece[...], full[...], preferred_element_type=jnp.float32
        ).astype(proj.dtype)


def query_kernel(scale, used, queries, full, proj, target, out, query_buf, full_buf, logits, sems):
    rows = [pl.ds(sum(PARTS[:i]), part) for i, part in enumerate(PARTS)]
    fetch = [
        pltpu.make_async_copy(queries.at[r], query_buf.at[r], sems.at[i])
        for i, r in enumerate(rows)
    ]
    load = pltpu.make_async_copy(full, full_buf, sems.at[len(PARTS)])
    load.start()
    fetch[0].start()
    load.wait()
    for i, r in enumerate(rows):
        fetch[i].wait()
        if i == 0:
            for copy in fetch[1:]:
                copy.start()
        query_proj = jnp.dot(
            query_buf[r, :], full_buf[...], preferred_element_type=jnp.float32
        ).astype(jnp.bfloat16)
        logits[:, r] = lax.dot_general(
            proj[...], query_proj, NT, preferred_element_type=jnp.float32
        )
        reduce_logits(scale, used, target, out, logits, r)


def reduce_logits(scale, used, target, out, logits, rows):
    tiles = logits.shape[0] // BLOCK
    sub = lax.broadcasted_iota(jnp.int32, (BLOCK, BLOCK), 0)
    for b in range(rows.start // BLOCK, (rows.start + rows.size) // BLOCK):
        lanes = pl.ds(b * BLOCK, BLOCK)
        live = [used[b, j] > 0 for j in range(tiles)]
        wanted = jnp.broadcast_to(target[b], (BLOCK, BLOCK)) - sub
        found = jnp.zeros((BLOCK, BLOCK), jnp.float32)
        top = jnp.full((8, BLOCK), FLOOR, jnp.float32)
        for j in range(tiles):
            tile = logits[pl.ds(j * BLOCK, BLOCK), lanes]
            found = found + jnp.where(wanted == j * BLOCK, tile, 0.0)
            peak = jnp.max(tile.reshape(BLOCK // 8, 8, BLOCK), axis=0)
            top = jnp.maximum(top, jnp.where(live[j], peak, FLOOR))
        found = jnp.sum(found, axis=0, keepdims=True) * scale
        top = jnp.max(top, axis=0, keepdims=True)
        acc = jnp.zeros((8, BLOCK), jnp.float32)
        for j in range(tiles):
            tile = logits[pl.ds(j * BLOCK, BLOCK), lanes]
            term = jnp.exp(jnp.where(live[j], tile - top, FLOOR) * scale)
            acc = acc + jnp.sum(term.reshape(BLOCK // 8, 8, BLOCK), axis=0)
        acc = jnp.sum(acc, axis=0, keepdims=True)
        some = acc > 0.0
        out[b, 0:1, :] = jnp.where(some, top * scale + jnp.log(jnp.where(some, acc, 1.0)), FLOOR)
        out[b, 1:2, :] = found


def local(queries, passages, head, positives, negative_ids, negative_count):
    queries, passages = queries[0], passages[0]
    width = queries.shape[1]
    scale = width ** (-0.5)
    deep = lax.axis_size("z")
    steps = lax.axis_size("y")
    z, high, low = lax.axis_index("z"), lax.axis_index("xh"), lax.axis_index("xl")
    core = lax.axis_index("core")
    rows = passages.shape[0]
    assert 4 * rows == width
    flip = [(0, 1), (1, 0)]
    both = [(0, 3), (1, 2), (2, 1), (3, 0)]

    gathered = lax.all_gather(queries, "z", axis=0, tiled=True)

    pieces = [
        passages,
        lax.ppermute(passages, "xl", flip),
        lax.ppermute(passages, "xh", flip),
        lax.ppermute(passages, ("xh", "xl"), both),
    ]
    mine = lax.all_to_all(jnp.broadcast_to(head, (steps,) + head.shape), "y", 0, 0)
    other = lax.ppermute(mine, "core", flip)

    slots = negative_ids.shape[2]
    alive = lax.broadcasted_iota(jnp.int32, (1, slots), 1) < negative_count
    listed = jnp.where(alive, negative_ids[0], -1)
    packed = jnp.concatenate(
        [positives, jnp.pad(listed, ((0, 0), (0, BLOCK - slots)), constant_values=-1)], axis=0
    )
    met_lists = lax.all_gather(packed, "z")
    wanted, lists = met_lists[:, 0, :], met_lists[:, 1, :slots]

    run = 2 * rows
    span = run * deep
    inside = wanted % span - z * run
    piece = 2 * ((wanted // span) ^ high) + ((inside // rows) ^ low)
    target = jnp.where((inside >= 0) & (inside < run), piece * rows + inside % rows, -1)
    tiles = rows // BLOCK
    tile = lax.iota(jnp.int32, 4 * tiles)
    piece = tile // tiles
    tile_id = ((((piece // 2) ^ high) * deep + z) * 2 + ((piece % 2) ^ low)) * tiles + tile % tiles
    used = jnp.any(lists[:, :, None] == tile_id[None, None, :], axis=1).astype(jnp.int32)

    vmem = pl.BlockSpec(memory_space=pltpu.VMEM)
    full, proj = pl.pallas_call(
        passage_kernel,
        out_shape=(jax.ShapeDtypeStruct((width, width), jnp.bfloat16),) * 2,
        in_specs=[pl.BlockSpec(memory_space=pltpu.SMEM)] + [vmem] * 6,
        out_specs=(vmem, vmem),
        compiler_params=pltpu.CompilerParams(vmem_limit_bytes=VMEM_BYTES),
    )(core[None], mine, other, *pieces)

    count = deep * queries.shape[0]
    hbm = pl.BlockSpec(memory_space=pltpu.HBM)
    in_hbm = functools.partial(pltpu.with_memory_space_constraint, memory_space=pltpu.HBM)
    stats = pl.pallas_call(
        functools.partial(query_kernel, scale),
        out_shape=jax.ShapeDtypeStruct((deep, 2, BLOCK), jnp.float32),
        in_specs=[pl.BlockSpec(memory_space=pltpu.SMEM), hbm, hbm, vmem, vmem],
        out_specs=vmem,
        scratch_shapes=[
            pltpu.VMEM((count, width), jnp.bfloat16),
            pltpu.VMEM((width, width), jnp.bfloat16),
            pltpu.VMEM((width, count), jnp.float32),
            pltpu.SemaphoreType.DMA((len(PARTS) + 1,)),
        ],
        compiler_params=pltpu.CompilerParams(vmem_limit_bytes=VMEM_BYTES),
    )(used, in_hbm(gathered), in_hbm(full), proj, target[:, None, :])

    home = lax.all_to_all(stats, "z", 0, 0)
    logit = jnp.sum(home[:, 1, :], axis=0)
    also_listed = jnp.any(listed[0][:, None] == positives // BLOCK, axis=0)
    extra = jnp.where(also_listed, FLOOR, logit)
    top = jnp.maximum(jnp.max(home[:, 0, :], axis=0), extra)
    total = jnp.sum(jnp.exp(home[:, 0, :] - top), axis=0) + jnp.exp(extra - top)
    return (top + jnp.log(total) - logit)[None, :]


def solution(mesh):
    grid = Mesh(mesh.devices.reshape(2, 12, 8, 2, 2), ("xh", "z", "y", "core", "xl"))
    shard, part = ("y", "core"), ("xh", "z", "xl")
    in_specs = (
        P(shard, part, None),
        P(shard, part, None),
        P(shard, None),
        P(shard, part),
        P(shard, part, None),
        P(shard, part),
    )
    return jax.shard_map(
        local, mesh=grid, in_specs=in_specs, out_specs=P(shard, part), check_vma=False
    )
```

```python
import functools

import jax
import jax.numpy as jnp
from jax import lax
from jax.experimental import pallas as pl
from jax.experimental.pallas import tpu as pltpu
from jax.sharding import Mesh
from jax.sharding import PartitionSpec as P

BLOCK = 128
FLOOR = -1e30
NT = (((1,), (1,)), ((), ()))
VMEM_BYTES = 24 * 1024 * 1024
PARTS = (512, 1024)


def passage_kernel(core, mine, other, *refs):
    *pieces, full, proj = refs
    steps, depth, _ = mine.shape
    here = core[0]
    for y in range(steps):
        first = pl.multiple_of((2 * y + here) * depth, depth)
        second = pl.multiple_of((2 * y + 1 - here) * depth, depth)
        full[pl.ds(first, depth), :] = mine[y]
        full[pl.ds(second, depth), :] = other[y]
    rows = pieces[0].shape[0]
    for s, piece in enumerate(pieces):
        proj[pl.ds(s * rows, rows), :] = jnp.dot(
            piece[...], full[...], preferred_element_type=jnp.float32
        ).astype(proj.dtype)


def query_kernel(scale, used, queries, full, proj, target, out, query_buf, proj_buf, logits, sems):
    rows = [pl.ds(sum(PARTS[:i]), part) for i, part in enumerate(PARTS)]
    fetch = [
        pltpu.make_async_copy(queries.at[r], query_buf.at[r], sems.at[i])
        for i, r in enumerate(rows)
    ]
    load = pltpu.make_async_copy(proj, proj_buf, sems.at[len(PARTS)])
    fetch[0].start()
    load.start()
    for copy in fetch[1:]:
        copy.start()
    for i, r in enumerate(rows):
        fetch[i].wait()
        query_proj = jnp.dot(
            query_buf[r, :], full[...], preferred_element_type=jnp.float32
        ).astype(jnp.bfloat16)
        if i == 0:
            load.wait()
        logits[:, r] = lax.dot_general(
            proj_buf[...], query_proj, NT, preferred_element_type=jnp.float32
        )
        reduce_logits(scale, used, target, out, logits, r)


def reduce_logits(scale, used, target, out, logits, rows):
    tiles = logits.shape[0] // BLOCK
    sub = lax.broadcasted_iota(jnp.int32, (BLOCK, BLOCK), 0)
    for b in range(rows.start // BLOCK, (rows.start + rows.size) // BLOCK):
        lanes = pl.ds(b * BLOCK, BLOCK)
        live = [used[b, j] > 0 for j in range(tiles)]
        wanted = jnp.broadcast_to(target[b], (BLOCK, BLOCK)) - sub
        found = jnp.zeros((BLOCK, BLOCK), jnp.float32)
        top = jnp.full((8, BLOCK), FLOOR, jnp.float32)
        for j in range(tiles):
            tile = logits[pl.ds(j * BLOCK, BLOCK), lanes]
            found = found + jnp.where(wanted == j * BLOCK, tile, 0.0)
            peak = jnp.max(tile.reshape(BLOCK // 8, 8, BLOCK), axis=0)
            top = jnp.maximum(top, jnp.where(live[j], peak, FLOOR))
        found = jnp.sum(found, axis=0, keepdims=True) * scale
        top = jnp.max(top, axis=0, keepdims=True)
        acc = jnp.zeros((8, BLOCK), jnp.float32)
        for j in range(tiles):
            tile = logits[pl.ds(j * BLOCK, BLOCK), lanes]
            term = jnp.exp(jnp.where(live[j], tile - top, FLOOR) * scale)
            acc = acc + jnp.sum(term.reshape(BLOCK // 8, 8, BLOCK), axis=0)
        acc = jnp.sum(acc, axis=0, keepdims=True)
        some = acc > 0.0
        out[b, 0:1, :] = jnp.where(some, top * scale + jnp.log(jnp.where(some, acc, 1.0)), FLOOR)
        out[b, 1:2, :] = found


def local(queries, passages, head, positives, negative_ids, negative_count):
    queries, passages = queries[0], passages[0]
    width = queries.shape[1]
    scale = width ** (-0.5)
    deep = lax.axis_size("z")
    steps = lax.axis_size("y")
    z, high, low = lax.axis_index("z"), lax.axis_index("xh"), lax.axis_index("xl")
    core = lax.axis_index("core")
    rows = passages.shape[0]
    assert 4 * rows == width
    flip = [(0, 1), (1, 0)]
    both = [(0, 3), (1, 2), (2, 1), (3, 0)]

    gathered = lax.all_gather(queries, "z", axis=0, tiled=True)

    pieces = [
        passages,
        lax.ppermute(passages, "xl", flip),
        lax.ppermute(passages, "xh", flip),
        lax.ppermute(passages, ("xh", "xl"), both),
    ]
    mine = lax.all_to_all(jnp.broadcast_to(head, (steps,) + head.shape), "y", 0, 0)
    other = lax.ppermute(mine, "core", flip)

    slots = negative_ids.shape[2]
    alive = lax.broadcasted_iota(jnp.int32, (1, slots), 1) < negative_count
    listed = jnp.where(alive, negative_ids[0], -1)
    packed = jnp.concatenate(
        [positives, jnp.pad(listed, ((0, 0), (0, BLOCK - slots)), constant_values=-1)], axis=0
    )
    met_lists = lax.all_to_all(jnp.broadcast_to(packed, (deep,) + packed.shape), "z", 0, 0)
    wanted, lists = met_lists[:, 0, :], met_lists[:, 1, :slots]

    run = 2 * rows
    span = run * deep
    inside = wanted % span - z * run
    piece = 2 * ((wanted // span) ^ high) + ((inside // rows) ^ low)
    target = jnp.where((inside >= 0) & (inside < run), piece * rows + inside % rows, -1)
    tiles = rows // BLOCK
    tile = lax.iota(jnp.int32, 4 * tiles)
    piece = tile // tiles
    tile_id = ((((piece // 2) ^ high) * deep + z) * 2 + ((piece % 2) ^ low)) * tiles + tile % tiles
    used = jnp.any(lists[:, :, None] == tile_id[None, None, :], axis=1).astype(jnp.int32)

    vmem = pl.BlockSpec(memory_space=pltpu.VMEM)
    full, proj = pl.pallas_call(
        passage_kernel,
        out_shape=(jax.ShapeDtypeStruct((width, width), jnp.bfloat16),) * 2,
        in_specs=[pl.BlockSpec(memory_space=pltpu.SMEM)] + [vmem] * 6,
        out_specs=(vmem, vmem),
        compiler_params=pltpu.CompilerParams(vmem_limit_bytes=VMEM_BYTES),
    )(core[None], mine, other, *pieces)

    count = deep * queries.shape[0]
    hbm = pl.BlockSpec(memory_space=pltpu.HBM)
    in_hbm = functools.partial(pltpu.with_memory_space_constraint, memory_space=pltpu.HBM)
    stats = pl.pallas_call(
        functools.partial(query_kernel, scale),
        out_shape=jax.ShapeDtypeStruct((deep, 2, BLOCK), jnp.float32),
        in_specs=[pl.BlockSpec(memory_space=pltpu.SMEM), hbm, vmem, hbm, vmem],
        out_specs=vmem,
        scratch_shapes=[
            pltpu.VMEM((count, width), jnp.bfloat16),
            pltpu.VMEM((width, width), jnp.bfloat16),
            pltpu.VMEM((width, count), jnp.float32),
            pltpu.SemaphoreType.DMA((len(PARTS) + 1,)),
        ],
        compiler_params=pltpu.CompilerParams(vmem_limit_bytes=VMEM_BYTES),
    )(used, in_hbm(gathered), full, in_hbm(proj), target[:, None, :])

    home = lax.all_to_all(stats, "z", 0, 0)
    logit = jnp.sum(home[:, 1, :], axis=0)
    also_listed = jnp.any(listed[0][:, None] == positives // BLOCK, axis=0)
    extra = jnp.where(also_listed, FLOOR, logit)
    top = jnp.maximum(jnp.max(home[:, 0, :], axis=0), extra)
    total = jnp.sum(jnp.exp(home[:, 0, :] - top), axis=0) + jnp.exp(extra - top)
    return (top + jnp.log(total) - logit)[None, :]


def solution(mesh):
    grid = Mesh(mesh.devices.reshape(2, 12, 8, 2, 2), ("xh", "z", "y", "core", "xl"))
    shard, part = ("y", "core"), ("xh", "z", "xl")
    in_specs = (
        P(shard, part, None),
        P(shard, part, None),
        P(shard, None),
        P(shard, part),
        P(shard, part, None),
        P(shard, part),
    )
    return jax.shard_map(
        local, mesh=grid, in_specs=in_specs, out_specs=P(shard, part), check_vma=False
    )
```

```python
import functools

import jax
import jax.numpy as jnp
from jax import lax
from jax.experimental import pallas as pl
from jax.experimental.pallas import tpu as pltpu
from jax.sharding import Mesh
from jax.sharding import PartitionSpec as P

BLOCK = 128
FLOOR = -1e30
NT = (((1,), (1,)), ((), ()))
VMEM_BYTES = 24 * 1024 * 1024


def passage_kernel(core, mine, other, p0, p1, p2, p3, proj, full, head_buf, piece_buf, sems):
    pieces = (p0, p1, p2, p3)
    heads = [
        pltpu.make_async_copy(half, head_buf.at[i], sems.at[i]) for i, half in enumerate((mine, other))
    ]
    loads = [
        pltpu.make_async_copy(piece, piece_buf.at[i], sems.at[2 + i])
        for i, piece in enumerate(pieces)
    ]
    for copy in heads + loads:
        copy.start()
    for copy in heads:
        copy.wait()
    steps, depth, _ = mine.shape
    here = core[0]
    for y in range(steps):
        first = pl.multiple_of((2 * y + here) * depth, depth)
        second = pl.multiple_of((2 * y + 1 - here) * depth, depth)
        full[pl.ds(first, depth), :] = head_buf[0, y]
        full[pl.ds(second, depth), :] = head_buf[1, y]
    for copy in loads:
        copy.wait()
    rows = p0.shape[0]
    for i in range(len(pieces)):
        proj[pl.ds(i * rows, rows), :] = jnp.dot(
            piece_buf[i], full[...], preferred_element_type=jnp.float32
        ).astype(proj.dtype)


def query_kernel(scale, turns, earlier, place, used, *refs):
    count = len(turns)
    blocks, (full, proj, target) = refs[:count], refs[count : count + 3]
    before, (out, query_buf, logits) = refs[count + 3 : -3], refs[-3:]
    for n, block in enumerate(blocks):
        query_buf[pl.ds(n * BLOCK, BLOCK), :] = block[...]
    query_proj = jnp.dot(
        query_buf[...], full[...], preferred_element_type=jnp.float32
    ).astype(jnp.bfloat16)
    logits[...] = lax.dot_general(proj[...], query_proj, NT, preferred_element_type=jnp.float32)
    for group, stats in zip(earlier, before):
        for n, turn in enumerate(group):
            out[place[turn]] = stats[n]
    tiles = logits.shape[0] // BLOCK
    sub = lax.broadcasted_iota(jnp.int32, (BLOCK, BLOCK), 0)
    for n, turn in enumerate(turns):
        b, lanes = place[turn], pl.ds(n * BLOCK, BLOCK)
        live = [used[b, j] > 0 for j in range(tiles)]
        wanted = jnp.broadcast_to(target[b], (BLOCK, BLOCK)) - sub
        found = jnp.zeros((BLOCK, BLOCK), jnp.float32)
        top = jnp.full((8, BLOCK), FLOOR, jnp.float32)
        for j in range(tiles):
            tile = logits[pl.ds(j * BLOCK, BLOCK), lanes]
            found = found + jnp.where(wanted == j * BLOCK, tile, 0.0)
            peak = jnp.max(tile.reshape(BLOCK // 8, 8, BLOCK), axis=0)
            top = jnp.maximum(top, jnp.where(live[j], peak, FLOOR))
        found = jnp.sum(found, axis=0, keepdims=True) * scale
        top = jnp.max(top, axis=0, keepdims=True)
        acc = jnp.zeros((8, BLOCK), jnp.float32)
        for j in range(tiles):
            tile = logits[pl.ds(j * BLOCK, BLOCK), lanes]
            term = jnp.exp(jnp.where(live[j], tile - top, FLOOR) * scale)
            acc = acc + jnp.sum(term.reshape(BLOCK // 8, 8, BLOCK), axis=0)
        acc = jnp.sum(acc, axis=0, keepdims=True)
        some = acc > 0.0
        lse = jnp.where(some, top * scale + jnp.log(jnp.where(some, acc, 1.0)), FLOOR)
        row = b if earlier else n
        out[row] = jnp.concatenate([lse, found], axis=0)


def local(queries, passages, head, positives, negative_ids, negative_count):
    queries, passages = queries[0], passages[0]
    width = queries.shape[1]
    scale = width ** (-0.5)
    deep = lax.axis_size("z")
    steps = lax.axis_size("y")
    z, high, low = lax.axis_index("z"), lax.axis_index("xh"), lax.axis_index("xl")
    core = lax.axis_index("core")
    rows = passages.shape[0]
    assert 4 * rows == width and queries.shape[0] == BLOCK
    flip = [(0, 1), (1, 0)]
    both = [(0, 3), (1, 2), (2, 1), (3, 0)]

    ahead = [(i, (i + 1) % deep) for i in range(deep)]
    back = [(i, (i - 1) % deep) for i in range(deep)]
    met = {0: queries}
    for turn in range(1, deep // 2 + 1):
        met[deep - turn] = lax.ppermute(met[(deep - turn + 1) % deep], "z", ahead)
        if 2 * turn < deep:
            met[turn] = lax.ppermute(met[turn - 1], "z", back)

    pieces = [
        passages,
        lax.ppermute(passages, "xl", flip),
        lax.ppermute(passages, "xh", flip),
        lax.ppermute(passages, ("xh", "xl"), both),
    ]
    mine = lax.all_to_all(jnp.broadcast_to(head, (steps,) + head.shape), "y", 0, 0)
    other = lax.ppermute(mine, "core", flip)

    slots = negative_ids.shape[2]
    alive = lax.broadcasted_iota(jnp.int32, (1, slots), 1) < negative_count
    listed = jnp.where(alive, negative_ids[0], -1)
    packed = jnp.concatenate(
        [positives, jnp.pad(listed, ((0, 0), (0, BLOCK - slots)), constant_values=-1)], axis=0
    )
    met_lists = lax.all_to_all(jnp.broadcast_to(packed, (deep,) + packed.shape), "z", 0, 0)
    wanted, lists = met_lists[:, 0, :], met_lists[:, 1, :slots]

    run = 2 * rows
    span = run * deep
    inside = wanted % span - z * run
    piece = 2 * ((wanted // span) ^ high) + ((inside // rows) ^ low)
    target = jnp.where((inside >= 0) & (inside < run), piece * rows + inside % rows, -1)
    tiles = rows // BLOCK
    tile = lax.iota(jnp.int32, 4 * tiles)
    piece = tile // tiles
    tile_id = ((((piece // 2) ^ high) * deep + z) * 2 + ((piece % 2) ^ low)) * tiles + tile % tiles
    used = jnp.any(lists[:, :, None] == tile_id[None, None, :], axis=1).astype(jnp.int32)

    vmem = pl.BlockSpec(memory_space=pltpu.VMEM)
    smem = pl.BlockSpec(memory_space=pltpu.SMEM)
    hbm = pl.BlockSpec(memory_space=pltpu.HBM)
    in_hbm = functools.partial(pltpu.with_memory_space_constraint, memory_space=pltpu.HBM)
    params = pltpu.CompilerParams(vmem_limit_bytes=VMEM_BYTES)
    square = jax.ShapeDtypeStruct((width, width), jnp.bfloat16)
    proj, full = pl.pallas_call(
        passage_kernel,
        out_shape=(square, square),
        in_specs=[smem] + [hbm] * 6,
        out_specs=(vmem, vmem),
        scratch_shapes=[
            pltpu.VMEM((2,) + mine.shape, jnp.bfloat16),
            pltpu.VMEM((4,) + passages.shape, jnp.bfloat16),
            pltpu.SemaphoreType.DMA((6,)),
        ],
        compiler_params=params,
        cost_estimate=pl.CostEstimate(flops=2 * width**3, transcendentals=0, bytes_accessed=8 * width**2),
    )(core[None], *map(in_hbm, (mine, other, *pieces)))

    place = (z + lax.iota(jnp.int32, deep)) % deep
    groups = [(0, deep - 1, 1)] + [(deep - t, t) for t in range(2, deep // 2)] + [(deep // 2,)]
    stats = []
    for group in groups:
        last = group is groups[-1]
        count = len(group)
        out = jax.ShapeDtypeStruct((deep if last else count, 2, BLOCK), jnp.float32)
        before = stats if last else []
        result = pl.pallas_call(
            functools.partial(query_kernel, scale, group, groups[:-1] if last else []),
            out_shape=out,
            in_specs=[smem, smem] + [vmem] * (count + 3 + len(before)),
            out_specs=vmem,
            scratch_shapes=[
                pltpu.VMEM((count * BLOCK, width), jnp.bfloat16),
                pltpu.VMEM((width, count * BLOCK), jnp.float32),
            ],
            compiler_params=params,
            cost_estimate=pl.CostEstimate(
                flops=4 * count * BLOCK * width**2,
                transcendentals=count * BLOCK * width,
                bytes_accessed=2 * count * BLOCK * width,
            ),
        )(place, used, *[met[t] for t in group], full, proj, target[:, None, :], *before)
        stats.append(result)
    stats = stats[-1]

    home = lax.all_to_all(stats, "z", 0, 0)
    logit = jnp.sum(home[:, 1, :], axis=0)
    also_listed = jnp.any(listed[0][:, None] == positives // BLOCK, axis=0)
    extra = jnp.where(also_listed, FLOOR, logit)
    top = jnp.maximum(jnp.max(home[:, 0, :], axis=0), extra)
    total = jnp.sum(jnp.exp(home[:, 0, :] - top), axis=0) + jnp.exp(extra - top)
    return (top + jnp.log(total) - logit)[None, :]


def solution(mesh):
    grid = Mesh(mesh.devices.reshape(2, 12, 8, 2, 2), ("xh", "z", "y", "core", "xl"))
    shard, part = ("y", "core"), ("xh", "z", "xl")
    in_specs = (
        P(shard, part, None),
        P(shard, part, None),
        P(shard, None),
        P(shard, part),
        P(shard, part, None),
        P(shard, part),
    )
    return jax.shard_map(
        local, mesh=grid, in_specs=in_specs, out_specs=P(shard, part), check_vma=False
    )
```

```python
import functools

import jax
import jax.numpy as jnp
from jax import lax
from jax.experimental import pallas as pl
from jax.experimental.pallas import tpu as pltpu
from jax.sharding import Mesh
from jax.sharding import PartitionSpec as P

BLOCK = 128
FLOOR = -1e30
NT = (((1,), (1,)), ((), ()))
VMEM_BYTES = 24 * 1024 * 1024
PARTS = (512, 1024)


def passage_kernel(core, mine, other, p0, p1, p2, p3, keys, full, proj, head_buf, piece_buf, sems):
    pieces = (p0, p1, p2, p3)
    heads = [
        pltpu.make_async_copy(half, head_buf.at[i], sems.at[i]) for i, half in enumerate((mine, other))
    ]
    loads = [
        pltpu.make_async_copy(piece, piece_buf.at[i], sems.at[2 + i])
        for i, piece in enumerate(pieces)
    ]
    for copy in heads + loads:
        copy.start()
    for copy in heads:
        copy.wait()
    steps, depth, _ = mine.shape
    here = core[0]
    for y in range(steps):
        first = pl.multiple_of((2 * y + here) * depth, depth)
        second = pl.multiple_of((2 * y + 1 - here) * depth, depth)
        full[pl.ds(first, depth), :] = head_buf[0, y]
        full[pl.ds(second, depth), :] = head_buf[1, y]
    for copy in loads:
        copy.wait()
    rows = p0.shape[0]
    for i in range(len(pieces)):
        proj[pl.ds(i * rows, rows), :] = jnp.dot(
            piece_buf[i], full[...], preferred_element_type=jnp.float32
        ).astype(proj.dtype)
    keys[...] = lax.dot_general(
        proj[...], full[...], NT, preferred_element_type=jnp.float32
    ).astype(keys.dtype)


def query_kernel(scale, used, queries, keys, target, out, query_buf, logits, sems):
    rows = [pl.ds(sum(PARTS[:i]), part) for i, part in enumerate(PARTS)]
    fetch = [
        pltpu.make_async_copy(queries.at[r], query_buf.at[r], sems.at[i])
        for i, r in enumerate(rows)
    ]
    for copy in fetch:
        copy.start()
    for copy, r in zip(fetch, rows):
        copy.wait()
        logits[:, r] = lax.dot_general(
            keys[...], query_buf[r, :], NT, preferred_element_type=jnp.float32
        )
        reduce_logits(scale, used, target, out, logits, r)


def reduce_logits(scale, used, target, out, logits, rows):
    tiles = logits.shape[0] // BLOCK
    sub = lax.broadcasted_iota(jnp.int32, (BLOCK, BLOCK), 0)
    for b in range(rows.start // BLOCK, (rows.start + rows.size) // BLOCK):
        lanes = pl.ds(b * BLOCK, BLOCK)
        live = [used[b, j] > 0 for j in range(tiles)]
        wanted = jnp.broadcast_to(target[b], (BLOCK, BLOCK)) - sub
        found = jnp.zeros((BLOCK, BLOCK), jnp.float32)
        top = jnp.full((8, BLOCK), FLOOR, jnp.float32)
        for j in range(tiles):
            tile = logits[pl.ds(j * BLOCK, BLOCK), lanes]
            found = found + jnp.where(wanted == j * BLOCK, tile, 0.0)
            peak = jnp.max(tile.reshape(BLOCK // 8, 8, BLOCK), axis=0)
            top = jnp.maximum(top, jnp.where(live[j], peak, FLOOR))
        found = jnp.sum(found, axis=0, keepdims=True) * scale
        top = jnp.max(top, axis=0, keepdims=True)
        acc = jnp.zeros((8, BLOCK), jnp.float32)
        for j in range(tiles):
            tile = logits[pl.ds(j * BLOCK, BLOCK), lanes]
            term = jnp.exp(jnp.where(live[j], tile - top, FLOOR) * scale)
            acc = acc + jnp.sum(term.reshape(BLOCK // 8, 8, BLOCK), axis=0)
        acc = jnp.sum(acc, axis=0, keepdims=True)
        some = acc > 0.0
        out[b, 0:1, :] = jnp.where(some, top * scale + jnp.log(jnp.where(some, acc, 1.0)), FLOOR)
        out[b, 1:2, :] = found


def local(queries, passages, head, positives, negative_ids, negative_count):
    queries, passages = queries[0], passages[0]
    width = queries.shape[1]
    scale = width ** (-0.5)
    deep = lax.axis_size("z")
    steps = lax.axis_size("y")
    z, high, low = lax.axis_index("z"), lax.axis_index("xh"), lax.axis_index("xl")
    core = lax.axis_index("core")
    rows = passages.shape[0]
    assert 4 * rows == width
    flip = [(0, 1), (1, 0)]
    both = [(0, 3), (1, 2), (2, 1), (3, 0)]

    gathered = lax.all_gather(queries, "z", axis=0, tiled=True)

    pieces = [
        passages,
        lax.ppermute(passages, "xl", flip),
        lax.ppermute(passages, "xh", flip),
        lax.ppermute(passages, ("xh", "xl"), both),
    ]
    mine = lax.all_to_all(jnp.broadcast_to(head, (steps,) + head.shape), "y", 0, 0)
    mine, *pieces = lax.optimization_barrier((mine, *pieces))
    other = lax.ppermute(mine, "core", flip)

    slots = negative_ids.shape[2]
    alive = lax.broadcasted_iota(jnp.int32, (1, slots), 1) < negative_count
    listed = jnp.where(alive, negative_ids[0], -1)
    packed = jnp.concatenate(
        [positives, jnp.pad(listed, ((0, 0), (0, BLOCK - slots)), constant_values=-1)], axis=0
    )
    vmem = pl.BlockSpec(memory_space=pltpu.VMEM)
    smem = pl.BlockSpec(memory_space=pltpu.SMEM)
    hbm = pl.BlockSpec(memory_space=pltpu.HBM)
    in_hbm = functools.partial(pltpu.with_memory_space_constraint, memory_space=pltpu.HBM)
    params = pltpu.CompilerParams(vmem_limit_bytes=VMEM_BYTES)
    keys = pl.pallas_call(
        passage_kernel,
        out_shape=jax.ShapeDtypeStruct((width, width), jnp.bfloat16),
        in_specs=[smem] + [hbm] * 6,
        out_specs=vmem,
        scratch_shapes=[
            pltpu.VMEM((width, width), jnp.bfloat16),
            pltpu.VMEM((width, width), jnp.bfloat16),
            pltpu.VMEM((2,) + mine.shape, jnp.bfloat16),
            pltpu.VMEM((4,) + passages.shape, jnp.bfloat16),
            pltpu.SemaphoreType.DMA((6,)),
        ],
        compiler_params=params,
    )(core[None], *map(in_hbm, (mine, other, *pieces)))

    met_lists = lax.all_to_all(jnp.broadcast_to(packed, (deep,) + packed.shape), "z", 0, 0)
    met_lists, keys = lax.optimization_barrier((met_lists, keys))
    wanted, lists = met_lists[:, 0, :], met_lists[:, 1, :slots]

    run = 2 * rows
    span = run * deep
    inside = wanted % span - z * run
    piece = 2 * ((wanted // span) ^ high) + ((inside // rows) ^ low)
    target = jnp.where((inside >= 0) & (inside < run), piece * rows + inside % rows, -1)
    tiles = rows // BLOCK
    tile = lax.iota(jnp.int32, 4 * tiles)
    piece = tile // tiles
    tile_id = ((((piece // 2) ^ high) * deep + z) * 2 + ((piece % 2) ^ low)) * tiles + tile % tiles
    used = jnp.any(lists[:, :, None] == tile_id[None, None, :], axis=1).astype(jnp.int32)

    count = deep * queries.shape[0]
    stats = pl.pallas_call(
        functools.partial(query_kernel, scale),
        out_shape=jax.ShapeDtypeStruct((deep, 2, BLOCK), jnp.float32),
        in_specs=[smem, hbm, vmem, vmem],
        out_specs=vmem,
        scratch_shapes=[
            pltpu.VMEM((count, width), jnp.bfloat16),
            pltpu.VMEM((width, count), jnp.float32),
            pltpu.SemaphoreType.DMA((len(PARTS),)),
        ],
        compiler_params=params,
    )(used, in_hbm(gathered), keys, target[:, None, :])

    home = lax.all_to_all(stats, "z", 0, 0)
    logit = jnp.sum(home[:, 1, :], axis=0)
    also_listed = jnp.any(listed[0][:, None] == positives // BLOCK, axis=0)
    extra = jnp.where(also_listed, FLOOR, logit)
    top = jnp.maximum(jnp.max(home[:, 0, :], axis=0), extra)
    total = jnp.sum(jnp.exp(home[:, 0, :] - top), axis=0) + jnp.exp(extra - top)
    return (top + jnp.log(total) - logit)[None, :]


def solution(mesh):
    grid = Mesh(mesh.devices.reshape(2, 12, 8, 2, 2), ("xh", "z", "y", "core", "xl"))
    shard, part = ("y", "core"), ("xh", "z", "xl")
    in_specs = (
        P(shard, part, None),
        P(shard, part, None),
        P(shard, None),
        P(shard, part),
        P(shard, part, None),
        P(shard, part),
    )
    return jax.shard_map(
        local, mesh=grid, in_specs=in_specs, out_specs=P(shard, part), check_vma=False
    )
```

```python
import functools

import jax
import jax.numpy as jnp
from jax import lax
from jax.experimental import pallas as pl
from jax.experimental.pallas import tpu as pltpu
from jax.sharding import Mesh
from jax.sharding import PartitionSpec as P

BLOCK = 128
FLOOR = -1e30
NT = (((1,), (1,)), ((), ()))
VMEM_BYTES = 24 * 1024 * 1024
PARTS = (512, 1024)


def passage_kernel(core, mine, other, p0, p1, p2, p3, keys, full, proj, head_buf, piece_buf, sems):
    pieces = (p0, p1, p2, p3)
    heads = [
        pltpu.make_async_copy(half, head_buf.at[i], sems.at[i]) for i, half in enumerate((mine, other))
    ]
    loads = [
        pltpu.make_async_copy(piece, piece_buf.at[i], sems.at[2 + i])
        for i, piece in enumerate(pieces)
    ]
    for copy in heads + loads:
        copy.start()
    for copy in heads:
        copy.wait()
    steps, depth, _ = mine.shape
    here = core[0]
    for y in range(steps):
        first = pl.multiple_of((2 * y + here) * depth, depth)
        second = pl.multiple_of((2 * y + 1 - here) * depth, depth)
        full[pl.ds(first, depth), :] = head_buf[0, y]
        full[pl.ds(second, depth), :] = head_buf[1, y]
    for copy in loads:
        copy.wait()
    rows = p0.shape[0]
    for i in range(len(pieces)):
        proj[pl.ds(i * rows, rows), :] = jnp.dot(
            piece_buf[i], full[...], preferred_element_type=jnp.float32
        ).astype(proj.dtype)
    keys[...] = lax.dot_general(
        proj[...], full[...], NT, preferred_element_type=jnp.float32
    ).astype(keys.dtype)


def query_kernel(scale, used, queries, keys, target, out, query_buf, logits, sems):
    rows = [pl.ds(sum(PARTS[:i]), part) for i, part in enumerate(PARTS)]
    fetch = [
        pltpu.make_async_copy(queries.at[r], query_buf.at[r], sems.at[i])
        for i, r in enumerate(rows)
    ]
    for copy in fetch:
        copy.start()
    for copy, r in zip(fetch, rows):
        copy.wait()
        logits[:, r] = lax.dot_general(
            keys[...], query_buf[r, :], NT, preferred_element_type=jnp.float32
        )
        reduce_logits(scale, used, target, out, logits, r)


def reduce_logits(scale, used, target, out, logits, rows):
    tiles = logits.shape[0] // BLOCK
    sub = lax.broadcasted_iota(jnp.int32, (BLOCK, BLOCK), 0)
    for b in range(rows.start // BLOCK, (rows.start + rows.size) // BLOCK):
        lanes = pl.ds(b * BLOCK, BLOCK)
        live = [used[b, j] > 0 for j in range(tiles)]
        wanted = jnp.broadcast_to(target[b], (BLOCK, BLOCK)) - sub
        found = jnp.zeros((BLOCK, BLOCK), jnp.float32)
        top = jnp.full((8, BLOCK), FLOOR, jnp.float32)
        for j in range(tiles):
            tile = logits[pl.ds(j * BLOCK, BLOCK), lanes]
            found = found + jnp.where(wanted == j * BLOCK, tile, 0.0)
            peak = jnp.max(tile.reshape(BLOCK // 8, 8, BLOCK), axis=0)
            top = jnp.maximum(top, jnp.where(live[j], peak, FLOOR))
        found = jnp.sum(found, axis=0, keepdims=True) * scale
        top = jnp.max(top, axis=0, keepdims=True)
        acc = jnp.zeros((8, BLOCK), jnp.float32)
        for j in range(tiles):
            tile = logits[pl.ds(j * BLOCK, BLOCK), lanes]
            term = jnp.exp(jnp.where(live[j], tile - top, FLOOR) * scale)
            acc = acc + jnp.sum(term.reshape(BLOCK // 8, 8, BLOCK), axis=0)
        acc = jnp.sum(acc, axis=0, keepdims=True)
        some = acc > 0.0
        out[b, 0:1, :] = jnp.where(some, top * scale + jnp.log(jnp.where(some, acc, 1.0)), FLOOR)
        out[b, 1:2, :] = found


def local(queries, passages, head, positives, negative_ids, negative_count):
    queries, passages = queries[0], passages[0]
    width = queries.shape[1]
    scale = width ** (-0.5)
    deep = lax.axis_size("z")
    steps = lax.axis_size("y")
    z, high, low = lax.axis_index("z"), lax.axis_index("xh"), lax.axis_index("xl")
    core = lax.axis_index("core")
    rows = passages.shape[0]
    assert 4 * rows == width
    flip = [(0, 1), (1, 0)]
    both = [(0, 3), (1, 2), (2, 1), (3, 0)]

    gathered = lax.all_gather(queries, "z", axis=0, tiled=True)

    pieces = [
        passages,
        lax.ppermute(passages, "xl", flip),
        lax.ppermute(passages, "xh", flip),
        lax.ppermute(passages, ("xh", "xl"), both),
    ]
    mine = lax.all_to_all(jnp.broadcast_to(head, (steps,) + head.shape), "y", 0, 0)
    slots = negative_ids.shape[2]
    alive = lax.broadcasted_iota(jnp.int32, (1, slots), 1) < negative_count
    listed = jnp.where(alive, negative_ids[0], -1)
    packed = jnp.concatenate(
        [positives, jnp.pad(listed, ((0, 0), (0, BLOCK - slots)), constant_values=-1)], axis=0
    )
    met_lists = lax.all_gather(packed, "z")
    mine, met_lists, *pieces = lax.optimization_barrier((mine, met_lists, *pieces))
    other = lax.ppermute(mine, "core", flip)

    vmem = pl.BlockSpec(memory_space=pltpu.VMEM)
    smem = pl.BlockSpec(memory_space=pltpu.SMEM)
    hbm = pl.BlockSpec(memory_space=pltpu.HBM)
    in_hbm = functools.partial(pltpu.with_memory_space_constraint, memory_space=pltpu.HBM)
    params = pltpu.CompilerParams(vmem_limit_bytes=VMEM_BYTES)
    keys = pl.pallas_call(
        passage_kernel,
        out_shape=jax.ShapeDtypeStruct((width, width), jnp.bfloat16),
        in_specs=[smem] + [hbm] * 6,
        out_specs=vmem,
        scratch_shapes=[
            pltpu.VMEM((width, width), jnp.bfloat16),
            pltpu.VMEM((width, width), jnp.bfloat16),
            pltpu.VMEM((2,) + mine.shape, jnp.bfloat16),
            pltpu.VMEM((4,) + passages.shape, jnp.bfloat16),
            pltpu.SemaphoreType.DMA((6,)),
        ],
        compiler_params=params,
    )(core[None], *map(in_hbm, (mine, other, *pieces)))

    wanted, lists = met_lists[:, 0, :], met_lists[:, 1, :slots]

    run = 2 * rows
    span = run * deep
    inside = wanted % span - z * run
    piece = 2 * ((wanted // span) ^ high) + ((inside // rows) ^ low)
    target = jnp.where((inside >= 0) & (inside < run), piece * rows + inside % rows, -1)
    tiles = rows // BLOCK
    tile = lax.iota(jnp.int32, 4 * tiles)
    piece = tile // tiles
    tile_id = ((((piece // 2) ^ high) * deep + z) * 2 + ((piece % 2) ^ low)) * tiles + tile % tiles
    used = jnp.any(lists[:, :, None] == tile_id[None, None, :], axis=1).astype(jnp.int32)

    count = deep * queries.shape[0]
    stats = pl.pallas_call(
        functools.partial(query_kernel, scale),
        out_shape=jax.ShapeDtypeStruct((deep, 2, BLOCK), jnp.float32),
        in_specs=[smem, hbm, vmem, vmem],
        out_specs=vmem,
        scratch_shapes=[
            pltpu.VMEM((count, width), jnp.bfloat16),
            pltpu.VMEM((width, count), jnp.float32),
            pltpu.SemaphoreType.DMA((len(PARTS),)),
        ],
        compiler_params=params,
    )(used, in_hbm(gathered), keys, target[:, None, :])

    home = lax.all_to_all(stats, "z", 0, 0)
    logit = jnp.sum(home[:, 1, :], axis=0)
    also_listed = jnp.any(listed[0][:, None] == positives // BLOCK, axis=0)
    extra = jnp.where(also_listed, FLOOR, logit)
    top = jnp.maximum(jnp.max(home[:, 0, :], axis=0), extra)
    total = jnp.sum(jnp.exp(home[:, 0, :] - top), axis=0) + jnp.exp(extra - top)
    return (top + jnp.log(total) - logit)[None, :]


def solution(mesh):
    grid = Mesh(mesh.devices.reshape(2, 12, 8, 2, 2), ("xh", "z", "y", "core", "xl"))
    shard, part = ("y", "core"), ("xh", "z", "xl")
    in_specs = (
        P(shard, part, None),
        P(shard, part, None),
        P(shard, None),
        P(shard, part),
        P(shard, part, None),
        P(shard, part),
    )
    return jax.shard_map(
        local, mesh=grid, in_specs=in_specs, out_specs=P(shard, part), check_vma=False
    )
```

```python
import functools

import jax
import jax.numpy as jnp
from jax import lax
from jax.experimental import pallas as pl
from jax.experimental.pallas import tpu as pltpu
from jax.sharding import Mesh
from jax.sharding import PartitionSpec as P

BLOCK = 128
FLOOR = -1e30
LOG2E = 1.4426950408889634
NT = (((1,), (1,)), ((), ()))
VMEM_BYTES = 24 * 1024 * 1024
PARTS = (512, 1024)


def passage_kernel(core, mine, other, p0, p1, p2, p3, keys, full, proj, head_buf, piece_buf, sems):
    pieces = (p0, p1, p2, p3)
    near = pltpu.make_async_copy(mine, head_buf, sems.at[0])
    loads = [
        pltpu.make_async_copy(piece, piece_buf.at[i], sems.at[1 + i])
        for i, piece in enumerate(pieces)
    ]
    for copy in [near] + loads:
        copy.start()
    near.wait()
    steps, depth, _ = mine.shape
    here = core[0]
    for y in range(steps):
        first = pl.multiple_of((2 * y + here) * depth, depth)
        second = pl.multiple_of((2 * y + 1 - here) * depth, depth)
        full[pl.ds(first, depth), :] = head_buf[y]
        full[pl.ds(second, depth), :] = other[y]
    for copy in loads:
        copy.wait()
    rows = p0.shape[0]
    for i in range(len(pieces)):
        proj[pl.ds(i * rows, rows), :] = jnp.dot(
            piece_buf[i], full[...], preferred_element_type=jnp.float32
        ).astype(proj.dtype)
    keys[...] = lax.dot_general(
        proj[...], full[...], NT, preferred_element_type=jnp.float32
    ).astype(keys.dtype)


def query_kernel(scale, used, queries, keys, target, out, query_buf, logits, sems):
    rows = [pl.ds(sum(PARTS[:i]), part) for i, part in enumerate(PARTS)]
    fetch = [
        pltpu.make_async_copy(queries.at[r], query_buf.at[r], sems.at[i])
        for i, r in enumerate(rows)
    ]
    for copy in fetch:
        copy.start()
    for copy, r in zip(fetch, rows):
        copy.wait()
        logits[:, r] = lax.dot_general(
            keys[...], query_buf[r, :], NT, preferred_element_type=jnp.float32
        )
        reduce_logits(scale, used, target, out, logits, r)


def reduce_logits(scale, used, target, out, logits, rows):
    tiles = logits.shape[0] // BLOCK
    sub = lax.broadcasted_iota(jnp.int32, (BLOCK, BLOCK), 0)
    for b in range(rows.start // BLOCK, (rows.start + rows.size) // BLOCK):
        lanes = pl.ds(b * BLOCK, BLOCK)
        live = [used[b, j] > 0 for j in range(tiles)]
        wanted = jnp.broadcast_to(target[b], (BLOCK, BLOCK)) - sub
        found = jnp.zeros((BLOCK, BLOCK), jnp.float32)
        top = jnp.full((8, BLOCK), FLOOR, jnp.float32)
        for j in range(tiles):
            tile = logits[pl.ds(j * BLOCK, BLOCK), lanes]
            found = found + jnp.where(wanted == j * BLOCK, tile, 0.0)
            peak = jnp.max(tile.reshape(BLOCK // 8, 8, BLOCK), axis=0)
            top = jnp.maximum(top, jnp.where(live[j], peak, FLOOR))
        found = jnp.sum(found, axis=0, keepdims=True) * scale
        top = jnp.max(top, axis=0, keepdims=True)
        acc = jnp.zeros((8, BLOCK), jnp.float32)
        for j in range(tiles):
            tile = logits[pl.ds(j * BLOCK, BLOCK), lanes]
            term = jnp.exp2((tile - jnp.where(live[j], top, -FLOOR)) * (scale * LOG2E))
            acc = acc + jnp.sum(term.reshape(BLOCK // 8, 8, BLOCK), axis=0)
        acc = jnp.sum(acc, axis=0, keepdims=True)
        some = acc > 0.0
        out[b, 0:1, :] = jnp.where(some, top * scale + jnp.log(jnp.where(some, acc, 1.0)), FLOOR)
        out[b, 1:2, :] = found


def local(queries, passages, head, positives, negative_ids, negative_count):
    queries, passages = queries[0], passages[0]
    width = queries.shape[1]
    scale = width ** (-0.5)
    deep = lax.axis_size("z")
    steps = lax.axis_size("y")
    z, high, low = lax.axis_index("z"), lax.axis_index("xh"), lax.axis_index("xl")
    core = lax.axis_index("core")
    rows = passages.shape[0]
    assert 4 * rows == width
    flip = [(0, 1), (1, 0)]
    both = [(0, 3), (1, 2), (2, 1), (3, 0)]

    gathered = lax.all_gather(queries, "z", axis=0, tiled=True)

    pieces = [
        passages,
        lax.ppermute(passages, "xl", flip),
        lax.ppermute(passages, "xh", flip),
        lax.ppermute(passages, ("xh", "xl"), both),
    ]
    mine = lax.all_to_all(jnp.broadcast_to(head, (steps,) + head.shape), "y", 0, 0)
    slots = negative_ids.shape[2]
    alive = lax.broadcasted_iota(jnp.int32, (1, slots), 1) < negative_count
    listed = jnp.where(alive, negative_ids[0], -1)
    packed = jnp.concatenate(
        [positives, jnp.pad(listed, ((0, 0), (0, BLOCK - slots)), constant_values=-1)], axis=0
    )
    met_lists = lax.all_gather(packed, "z")
    mine, met_lists, *pieces = lax.optimization_barrier((mine, met_lists, *pieces))
    other = lax.ppermute(mine, "core", flip)

    vmem = pl.BlockSpec(memory_space=pltpu.VMEM)
    smem = pl.BlockSpec(memory_space=pltpu.SMEM)
    hbm = pl.BlockSpec(memory_space=pltpu.HBM)
    in_hbm = functools.partial(pltpu.with_memory_space_constraint, memory_space=pltpu.HBM)
    params = pltpu.CompilerParams(vmem_limit_bytes=VMEM_BYTES)
    keys = pl.pallas_call(
        passage_kernel,
        out_shape=jax.ShapeDtypeStruct((width, width), jnp.bfloat16),
        in_specs=[smem, hbm, vmem] + [hbm] * 4,
        out_specs=vmem,
        scratch_shapes=[
            pltpu.VMEM((width, width), jnp.bfloat16),
            pltpu.VMEM((width, width), jnp.bfloat16),
            pltpu.VMEM(mine.shape, jnp.bfloat16),
            pltpu.VMEM((4,) + passages.shape, jnp.bfloat16),
            pltpu.SemaphoreType.DMA((5,)),
        ],
        compiler_params=params,
    )(core[None], in_hbm(mine), other, *map(in_hbm, pieces))

    wanted, lists = met_lists[:, 0, :], met_lists[:, 1, :slots]

    run = 2 * rows
    span = run * deep
    inside = wanted % span - z * run
    piece = 2 * ((wanted // span) ^ high) + ((inside // rows) ^ low)
    target = jnp.where((inside >= 0) & (inside < run), piece * rows + inside % rows, -1)
    tiles = rows // BLOCK
    tile = lax.iota(jnp.int32, 4 * tiles)
    piece = tile // tiles
    tile_id = ((((piece // 2) ^ high) * deep + z) * 2 + ((piece % 2) ^ low)) * tiles + tile % tiles
    used = jnp.any(lists[:, :, None] == tile_id[None, None, :], axis=1).astype(jnp.int32)

    also_listed = jnp.any(listed[0][:, None] == positives // BLOCK, axis=0).astype(jnp.int32)
    used, also_listed = lax.optimization_barrier((used, also_listed))
    count = deep * queries.shape[0]
    stats = pl.pallas_call(
        functools.partial(query_kernel, scale),
        out_shape=jax.ShapeDtypeStruct((deep, 2, BLOCK), jnp.float32),
        in_specs=[smem, hbm, vmem, vmem],
        out_specs=vmem,
        scratch_shapes=[
            pltpu.VMEM((count, width), jnp.bfloat16),
            pltpu.VMEM((width, count), jnp.float32),
            pltpu.SemaphoreType.DMA((len(PARTS),)),
        ],
        compiler_params=params,
    )(used, in_hbm(gathered), keys, target[:, None, :])

    home = lax.all_to_all(stats, "z", 0, 0)
    logit = jnp.sum(home[:, 1, :], axis=0)
    extra = jnp.where(also_listed > 0, FLOOR, logit)
    top = jnp.maximum(jnp.max(home[:, 0, :], axis=0), extra)
    total = jnp.sum(jnp.exp(home[:, 0, :] - top), axis=0) + jnp.exp(extra - top)
    return (top + jnp.log(total) - logit)[None, :]


def solution(mesh):
    grid = Mesh(mesh.devices.reshape(2, 12, 8, 2, 2), ("xh", "z", "y", "core", "xl"))
    shard, part = ("y", "core"), ("xh", "z", "xl")
    in_specs = (
        P(shard, part, None),
        P(shard, part, None),
        P(shard, None),
        P(shard, part),
        P(shard, part, None),
        P(shard, part),
    )
    return jax.shard_map(
        local, mesh=grid, in_specs=in_specs, out_specs=P(shard, part), check_vma=False
    )
```

```python
import functools

import jax
import jax.numpy as jnp
from jax import lax
from jax.experimental import pallas as pl
from jax.experimental.pallas import tpu as pltpu
from jax.sharding import Mesh
from jax.sharding import PartitionSpec as P

BLOCK = 128
FLOOR = -1e30
LOG2E = 1.4426950408889634
NT = (((1,), (1,)), ((), ()))
VMEM_BYTES = 24 * 1024 * 1024
PARTS = (512, 1024)


def passage_kernel(core, mine, other, p0, p1, p2, p3, keys, full, proj, head_buf, piece_buf, sems):
    pieces = (p0, p1, p2, p3)
    near = pltpu.make_async_copy(mine, head_buf, sems.at[0])
    loads = [
        pltpu.make_async_copy(piece, piece_buf.at[i], sems.at[1 + i])
        for i, piece in enumerate(pieces)
    ]
    for copy in [near] + loads:
        copy.start()
    near.wait()
    steps, depth, _ = mine.shape
    here = core[0]
    for y in range(steps):
        first = pl.multiple_of((2 * y + here) * depth, depth)
        second = pl.multiple_of((2 * y + 1 - here) * depth, depth)
        full[pl.ds(first, depth), :] = head_buf[y]
        full[pl.ds(second, depth), :] = other[y]
    for copy in loads:
        copy.wait()
    proj[...] = jnp.dot(
        piece_buf[...].reshape(proj.shape), full[...], preferred_element_type=jnp.float32
    ).astype(proj.dtype)
    keys[...] = lax.dot_general(
        proj[...], full[...], NT, preferred_element_type=jnp.float32
    ).astype(keys.dtype)


def query_kernel(scale, used, queries, keys, target, out, query_buf, logits, sems):
    rows = [pl.ds(sum(PARTS[:i]), part) for i, part in enumerate(PARTS)]
    fetch = [
        pltpu.make_async_copy(queries.at[r], query_buf.at[r], sems.at[i])
        for i, r in enumerate(rows)
    ]
    for copy in fetch:
        copy.start()
    for copy, r in zip(fetch, rows):
        copy.wait()
        logits[:, r] = lax.dot_general(
            keys[...], query_buf[r, :], NT, preferred_element_type=jnp.float32
        )
        reduce_logits(scale, used, target, out, logits, r)


def reduce_logits(scale, used, target, out, logits, rows):
    tiles = logits.shape[0] // BLOCK
    sub = lax.broadcasted_iota(jnp.int32, (BLOCK, BLOCK), 0)
    for b in range(rows.start // BLOCK, (rows.start + rows.size) // BLOCK):
        lanes = pl.ds(b * BLOCK, BLOCK)
        live = [used[b, j] > 0 for j in range(tiles)]
        wanted = jnp.broadcast_to(target[b], (BLOCK, BLOCK)) - sub
        found = jnp.zeros((BLOCK, BLOCK), jnp.float32)
        top = jnp.full((8, BLOCK), FLOOR, jnp.float32)
        for j in range(tiles):
            tile = logits[pl.ds(j * BLOCK, BLOCK), lanes]
            found = found + jnp.where(wanted == j * BLOCK, tile, 0.0)
            peak = jnp.max(tile.reshape(BLOCK // 8, 8, BLOCK), axis=0)
            top = jnp.maximum(top, jnp.where(live[j], peak, FLOOR))
        found = jnp.sum(found, axis=0, keepdims=True) * scale
        top = jnp.max(top, axis=0, keepdims=True)
        acc = jnp.zeros((8, BLOCK), jnp.float32)
        for j in range(tiles):
            tile = logits[pl.ds(j * BLOCK, BLOCK), lanes]
            term = jnp.exp2((tile - jnp.where(live[j], top, -FLOOR)) * (scale * LOG2E))
            acc = acc + jnp.sum(term.reshape(BLOCK // 8, 8, BLOCK), axis=0)
        acc = jnp.sum(acc, axis=0, keepdims=True)
        some = acc > 0.0
        out[b, 0:1, :] = jnp.where(some, top * scale + jnp.log(jnp.where(some, acc, 1.0)), FLOOR)
        out[b, 1:2, :] = found


def local(queries, passages, head, positives, negative_ids, negative_count):
    queries, passages = queries[0], passages[0]
    width = queries.shape[1]
    scale = width ** (-0.5)
    deep = lax.axis_size("z")
    steps = lax.axis_size("y")
    z, high, low = lax.axis_index("z"), lax.axis_index("xh"), lax.axis_index("xl")
    core = lax.axis_index("core")
    rows = passages.shape[0]
    assert 4 * rows == width
    flip = [(0, 1), (1, 0)]
    both = [(0, 3), (1, 2), (2, 1), (3, 0)]

    gathered = lax.all_gather(queries, "z", axis=0, tiled=True)

    pieces = [
        passages,
        lax.ppermute(passages, "xl", flip),
        lax.ppermute(passages, "xh", flip),
        lax.ppermute(passages, ("xh", "xl"), both),
    ]
    mine = lax.all_to_all(jnp.broadcast_to(head, (steps,) + head.shape), "y", 0, 0)
    slots = negative_ids.shape[2]
    alive = lax.broadcasted_iota(jnp.int32, (1, slots), 1) < negative_count
    listed = jnp.where(alive, negative_ids[0], -1)
    packed = jnp.concatenate(
        [positives, jnp.pad(listed, ((0, 0), (0, BLOCK - slots)), constant_values=-1)], axis=0
    )
    met_lists = lax.all_gather(packed, "z")
    mine, met_lists, *pieces = lax.optimization_barrier((mine, met_lists, *pieces))
    other = lax.ppermute(mine, "core", flip)

    vmem = pl.BlockSpec(memory_space=pltpu.VMEM)
    smem = pl.BlockSpec(memory_space=pltpu.SMEM)
    hbm = pl.BlockSpec(memory_space=pltpu.HBM)
    in_hbm = functools.partial(pltpu.with_memory_space_constraint, memory_space=pltpu.HBM)
    params = pltpu.CompilerParams(vmem_limit_bytes=VMEM_BYTES)
    keys = pl.pallas_call(
        passage_kernel,
        out_shape=jax.ShapeDtypeStruct((width, width), jnp.bfloat16),
        in_specs=[smem, hbm, vmem] + [hbm] * 4,
        out_specs=vmem,
        scratch_shapes=[
            pltpu.VMEM((width, width), jnp.bfloat16),
            pltpu.VMEM((width, width), jnp.bfloat16),
            pltpu.VMEM(mine.shape, jnp.bfloat16),
            pltpu.VMEM((4,) + passages.shape, jnp.bfloat16),
            pltpu.SemaphoreType.DMA((5,)),
        ],
        compiler_params=params,
    )(core[None], in_hbm(mine), other, *map(in_hbm, pieces))

    wanted, lists = met_lists[:, 0, :], met_lists[:, 1, :slots]

    run = 2 * rows
    span = run * deep
    inside = wanted % span - z * run
    piece = 2 * ((wanted // span) ^ high) + ((inside // rows) ^ low)
    target = jnp.where((inside >= 0) & (inside < run), piece * rows + inside % rows, -1)
    tiles = rows // BLOCK
    tile = lax.iota(jnp.int32, 4 * tiles)
    piece = tile // tiles
    tile_id = ((((piece // 2) ^ high) * deep + z) * 2 + ((piece % 2) ^ low)) * tiles + tile % tiles
    used = jnp.any(lists[:, :, None] == tile_id[None, None, :], axis=1).astype(jnp.int32)

    also_listed = jnp.any(listed[0][:, None] == positives // BLOCK, axis=0).astype(jnp.int32)
    used, also_listed = lax.optimization_barrier((used, also_listed))
    count = deep * queries.shape[0]
    stats = pl.pallas_call(
        functools.partial(query_kernel, scale),
        out_shape=jax.ShapeDtypeStruct((deep, 2, BLOCK), jnp.float32),
        in_specs=[smem, hbm, vmem, vmem],
        out_specs=vmem,
        scratch_shapes=[
            pltpu.VMEM((count, width), jnp.bfloat16),
            pltpu.VMEM((width, count), jnp.float32),
            pltpu.SemaphoreType.DMA((len(PARTS),)),
        ],
        compiler_params=params,
    )(used, in_hbm(gathered), keys, target[:, None, :])

    home = lax.all_to_all(stats, "z", 0, 0)
    logit = jnp.sum(home[:, 1, :], axis=0)
    extra = jnp.where(also_listed > 0, FLOOR, logit)
    top = jnp.maximum(jnp.max(home[:, 0, :], axis=0), extra)
    total = jnp.sum(jnp.exp(home[:, 0, :] - top), axis=0) + jnp.exp(extra - top)
    return (top + jnp.log(total) - logit)[None, :]


def solution(mesh):
    grid = Mesh(mesh.devices.reshape(2, 12, 8, 2, 2), ("xh", "z", "y", "core", "xl"))
    shard, part = ("y", "core"), ("xh", "z", "xl")
    in_specs = (
        P(shard, part, None),
        P(shard, part, None),
        P(shard, None),
        P(shard, part),
        P(shard, part, None),
        P(shard, part),
    )
    return jax.shard_map(
        local, mesh=grid, in_specs=in_specs, out_specs=P(shard, part), check_vma=False
    )
```

```python
import functools

import jax
import jax.numpy as jnp
from jax import lax
from jax.experimental import pallas as pl
from jax.experimental.pallas import tpu as pltpu
from jax.sharding import Mesh
from jax.sharding import PartitionSpec as P

BLOCK = 128
FLOOR = -1e30
LOG2E = 1.4426950408889634
NT = (((1,), (1,)), ((), ()))
VMEM_BYTES = 24 * 1024 * 1024
PARTS = (512, 1024)


def copy_kernel(head, copies):
    for y in range(copies.shape[0]):
        copies[y] = head[...]


def passage_kernel(core, mine, other, p0, p1, p2, p3, keys, full, proj, head_buf, piece_buf, sems):
    pieces = (p0, p1, p2, p3)
    near = pltpu.make_async_copy(mine, head_buf, sems.at[0])
    loads = [
        pltpu.make_async_copy(piece, piece_buf.at[i], sems.at[1 + i])
        for i, piece in enumerate(pieces)
    ]
    for copy in [near] + loads:
        copy.start()
    near.wait()
    steps, depth, _ = mine.shape
    here = core[0]
    for y in range(steps):
        first = pl.multiple_of((2 * y + here) * depth, depth)
        second = pl.multiple_of((2 * y + 1 - here) * depth, depth)
        full[pl.ds(first, depth), :] = head_buf[y]
        full[pl.ds(second, depth), :] = other[y]
    for copy in loads:
        copy.wait()
    rows = p0.shape[0]
    for i in range(len(pieces)):
        proj[pl.ds(i * rows, rows), :] = jnp.dot(
            piece_buf[i], full[...], preferred_element_type=jnp.float32
        ).astype(proj.dtype)
    keys[...] = lax.dot_general(
        proj[...], full[...], NT, preferred_element_type=jnp.float32
    ).astype(keys.dtype)


def query_kernel(scale, used, queries, keys, target, out, query_buf, logits, sems):
    rows = [pl.ds(sum(PARTS[:i]), part) for i, part in enumerate(PARTS)]
    fetch = [
        pltpu.make_async_copy(queries.at[r], query_buf.at[r], sems.at[i])
        for i, r in enumerate(rows)
    ]
    for copy in fetch:
        copy.start()
    for copy, r in zip(fetch, rows):
        copy.wait()
        logits[:, r] = lax.dot_general(
            keys[...], query_buf[r, :], NT, preferred_element_type=jnp.float32
        )
        reduce_logits(scale, used, target, out, logits, r)


def reduce_logits(scale, used, target, out, logits, rows):
    tiles = logits.shape[0] // BLOCK
    sub = lax.broadcasted_iota(jnp.int32, (BLOCK, BLOCK), 0)
    for b in range(rows.start // BLOCK, (rows.start + rows.size) // BLOCK):
        lanes = pl.ds(b * BLOCK, BLOCK)
        live = [used[b, j] > 0 for j in range(tiles)]
        wanted = jnp.broadcast_to(target[b], (BLOCK, BLOCK)) - sub
        found = jnp.zeros((BLOCK, BLOCK), jnp.float32)
        top = jnp.full((8, BLOCK), FLOOR, jnp.float32)
        for j in range(tiles):
            tile = logits[pl.ds(j * BLOCK, BLOCK), lanes]
            found = found + jnp.where(wanted == j * BLOCK, tile, 0.0)
            peak = jnp.max(tile.reshape(BLOCK // 8, 8, BLOCK), axis=0)
            top = jnp.maximum(top, jnp.where(live[j], peak, FLOOR))
        found = jnp.sum(found, axis=0, keepdims=True) * scale
        top = jnp.max(top, axis=0, keepdims=True)
        acc = jnp.zeros((8, BLOCK), jnp.float32)
        for j in range(tiles):
            tile = logits[pl.ds(j * BLOCK, BLOCK), lanes]
            term = jnp.exp2((tile - jnp.where(live[j], top, -FLOOR)) * (scale * LOG2E))
            acc = acc + jnp.sum(term.reshape(BLOCK // 8, 8, BLOCK), axis=0)
        acc = jnp.sum(acc, axis=0, keepdims=True)
        some = acc > 0.0
        out[b, 0:1, :] = jnp.where(some, top * scale + jnp.log(jnp.where(some, acc, 1.0)), FLOOR)
        out[b, 1:2, :] = found


def local(queries, passages, head, positives, negative_ids, negative_count):
    queries, passages = queries[0], passages[0]
    width = queries.shape[1]
    scale = width ** (-0.5)
    deep = lax.axis_size("z")
    steps = lax.axis_size("y")
    z, high, low = lax.axis_index("z"), lax.axis_index("xh"), lax.axis_index("xl")
    core = lax.axis_index("core")
    rows = passages.shape[0]
    assert 4 * rows == width
    flip = [(0, 1), (1, 0)]
    both = [(0, 3), (1, 2), (2, 1), (3, 0)]

    gathered = lax.all_gather(queries, "z", axis=0, tiled=True)

    pieces = [
        passages,
        lax.ppermute(passages, "xl", flip),
        lax.ppermute(passages, "xh", flip),
        lax.ppermute(passages, ("xh", "xl"), both),
    ]
    mine = lax.all_to_all(
        pl.pallas_call(
            copy_kernel,
            out_shape=jax.ShapeDtypeStruct((steps,) + head.shape, head.dtype),
            in_specs=[pl.BlockSpec(memory_space=pltpu.VMEM)],
            out_specs=pl.BlockSpec(memory_space=pltpu.VMEM),
        )(head),
        "y",
        0,
        0,
    )
    slots = negative_ids.shape[2]
    alive = lax.broadcasted_iota(jnp.int32, (1, slots), 1) < negative_count
    listed = jnp.where(alive, negative_ids[0], -1)
    packed = jnp.concatenate(
        [positives, jnp.pad(listed, ((0, 0), (0, BLOCK - slots)), constant_values=-1)], axis=0
    )
    met_lists = lax.all_gather(packed, "z")
    mine, met_lists, *pieces = lax.optimization_barrier((mine, met_lists, *pieces))
    other = lax.ppermute(mine, "core", flip)

    vmem = pl.BlockSpec(memory_space=pltpu.VMEM)
    smem = pl.BlockSpec(memory_space=pltpu.SMEM)
    hbm = pl.BlockSpec(memory_space=pltpu.HBM)
    in_hbm = functools.partial(pltpu.with_memory_space_constraint, memory_space=pltpu.HBM)
    params = pltpu.CompilerParams(vmem_limit_bytes=VMEM_BYTES)
    keys = pl.pallas_call(
        passage_kernel,
        out_shape=jax.ShapeDtypeStruct((width, width), jnp.bfloat16),
        in_specs=[smem, hbm, vmem] + [hbm] * 4,
        out_specs=vmem,
        scratch_shapes=[
            pltpu.VMEM((width, width), jnp.bfloat16),
            pltpu.VMEM((width, width), jnp.bfloat16),
            pltpu.VMEM(mine.shape, jnp.bfloat16),
            pltpu.VMEM((4,) + passages.shape, jnp.bfloat16),
            pltpu.SemaphoreType.DMA((5,)),
        ],
        compiler_params=params,
    )(core[None], in_hbm(mine), other, *map(in_hbm, pieces))

    wanted, lists = met_lists[:, 0, :], met_lists[:, 1, :slots]

    run = 2 * rows
    span = run * deep
    inside = wanted % span - z * run
    piece = 2 * ((wanted // span) ^ high) + ((inside // rows) ^ low)
    target = jnp.where((inside >= 0) & (inside < run), piece * rows + inside % rows, -1)
    tiles = rows // BLOCK
    tile = lax.iota(jnp.int32, 4 * tiles)
    piece = tile // tiles
    tile_id = ((((piece // 2) ^ high) * deep + z) * 2 + ((piece % 2) ^ low)) * tiles + tile % tiles
    used = jnp.any(lists[:, :, None] == tile_id[None, None, :], axis=1).astype(jnp.int32)

    also_listed = jnp.any(listed[0][:, None] == positives // BLOCK, axis=0).astype(jnp.int32)
    used, also_listed = lax.optimization_barrier((used, also_listed))
    count = deep * queries.shape[0]
    stats = pl.pallas_call(
        functools.partial(query_kernel, scale),
        out_shape=jax.ShapeDtypeStruct((deep, 2, BLOCK), jnp.float32),
        in_specs=[smem, hbm, vmem, vmem],
        out_specs=vmem,
        scratch_shapes=[
            pltpu.VMEM((count, width), jnp.bfloat16),
            pltpu.VMEM((width, count), jnp.float32),
            pltpu.SemaphoreType.DMA((len(PARTS),)),
        ],
        compiler_params=params,
    )(used, in_hbm(gathered), keys, target[:, None, :])

    home = lax.all_to_all(stats, "z", 0, 0)
    logit = jnp.sum(home[:, 1, :], axis=0)
    extra = jnp.where(also_listed > 0, FLOOR, logit)
    top = jnp.maximum(jnp.max(home[:, 0, :], axis=0), extra)
    total = jnp.sum(jnp.exp(home[:, 0, :] - top), axis=0) + jnp.exp(extra - top)
    return (top + jnp.log(total) - logit)[None, :]


def solution(mesh):
    grid = Mesh(mesh.devices.reshape(2, 12, 8, 2, 2), ("xh", "z", "y", "core", "xl"))
    shard, part = ("y", "core"), ("xh", "z", "xl")
    in_specs = (
        P(shard, part, None),
        P(shard, part, None),
        P(shard, None),
        P(shard, part),
        P(shard, part, None),
        P(shard, part),
    )
    return jax.shard_map(
        local, mesh=grid, in_specs=in_specs, out_specs=P(shard, part), check_vma=False
    )
```
